32 devices in a mesh: rep: 4 (over x, core), row: 4 (over z), col: 2 (over y).
Axes of the slice: x: 2, y: 2, z: 4, core: 2. Of those that a mesh axis runs over, the one named last changes fastest.
Arguments:
- inputs: bfloat16 [4, 128, 6144], P('rep', 'col', 'row'), may hold values from -6 to 6
- w_in: bfloat16 [6144, 24576], P('row', ('rep', 'col')), may hold values from -0.078125 to 0.078125
- w_out: bfloat16 [24576, 6144], P(('rep', 'col'), 'row'), may hold values from -0.0390625 to 0.0390625
- cotangent: bfloat16 [4, 128, 6144], P('rep', 'col', 'row'), may hold values from -1536 to 1536
- counts: int32 [4], replicated, may hold values from 0 to 4, as said below
Outputs:
- block_output: bfloat16 [4, 128, 6144], P('rep', 'col', 'row')
- input_grad: bfloat16 [4, 128, 6144], P('rep', 'col', 'row')
- w_in_grad: float32 [6144, 24576], P('row', ('rep', 'col'))
- w_out_grad: float32 [24576, 6144], P(('rep', 'col'), 'row')
The draws below stay inside these ranges and needn't reach their ends.
Inputs may be any that keep to these rules, and one draw needn't show every extreme that they name: Replica r completed its first counts[r] micro-batches; at least one replica completed all 4.
All inputs are finite; a program needn't handle non-finite values.
Results may differ from the reference program's by a relative error of at most 0.015.
Values may be sent and summed in bfloat16 or wider, within the bound.
A program may use at most 192 MiB of HBM per device.

```python
import jax
import jax.numpy as jnp

D = 6144
FF = 24576
MB = 4
MBT = 32
TOKENS = 128
N_REP = 4
N_ROW = 4
N_COL = 2


def draw_counts(key, part):
    first = jax.random.fold_in(key, 11)
    second = jax.random.fold_in(key, 23)
    values = jax.random.randint(first, (N_REP,), 0, MB + 1)
    chosen = jax.random.randint(second, (), 0, N_REP)
    return jnp.where(jnp.arange(N_REP) == chosen, MB, values).astype(jnp.int32)


def block_scale(stream_key, dims, cuts, least, top_value):
    level, own = 1.0, jax.random.fold_in(stream_key, 6)
    for axis_at, blocks in cuts:
        steps = jnp.exp(jax.random.uniform(jax.random.fold_in(own, axis_at), (blocks,), jnp.float32, least / len(cuts), top_value / len(cuts)))
        level = level * jnp.repeat(steps, dims[axis_at] // blocks).reshape([-1 if axis == axis_at else 1 for axis in range(len(dims))])
    return level


def noise(rng, dims, spread, most, shards=(), held_as=jnp.bfloat16):
    array = jax.random.normal(rng, dims, jnp.float32) * spread
    if len(shards) > 0:
        array = block_scale(rng, dims, shards, -0.22, 0.18) * array
    return jnp.clip(array, min=-most, max=most).astype(held_as)


def setup_inputs(seed: int = 0) -> dict:
    streams_of = jax.random.split(jax.random.key(seed), 6)
    return {
        "inputs": noise(streams_of[0], (N_REP, TOKENS, D), 1.0, 6.0, ((0, 4), (1, 2), (2, 4))),
        "w_in": noise(streams_of[1], (D, FF), D ** -0.5, 0.078125, ((0, 4), (1, 8))),
        "w_out": noise(streams_of[2], (FF, D), FF ** -0.5, 0.0390625, ((0, 8), (1, 4))),
        "cotangent": noise(streams_of[3], (N_REP, TOKENS, D), (MBT * MB * N_REP // 2), 1536.0, ((0, 4), (1, 2), (2, 4))),
        "counts": draw_counts(jax.random.fold_in(streams_of[5], 71), 0),
    }


root_coef = 0.7978845608028654
cubic_coef = 0.044715


def gelu_tanh(values):
    inner = root_coef * (values + cubic_coef * values * values * values)
    return 0.5 * values * (1.0 + jnp.tanh(inner))


def gelu_slope(values):
    inner = root_coef * (values + cubic_coef * values * values * values)
    tangent = jnp.tanh(inner)
    return 0.5 * (1.0 + tangent) + 0.5 * values * (1.0 - tangent * tangent) * root_coef * (1.0 + 3.0 * cubic_coef * values * values)


def rounded_term(left, right):
    return jnp.dot(left, right, preferred_element_type=jnp.float32).astype(jnp.bfloat16).astype(jnp.float32)


def block_sum(left, right):
    width = left.shape[1] // N_ROW
    total = jnp.zeros((left.shape[0], right.shape[1]), jnp.float32)
    for block in range(N_ROW):
        total = total + rounded_term(left[:, block * width:(block + 1) * width], right[block * width:(block + 1) * width, :])
    return total


def set_sum(left, right):
    piece = FF // (N_REP * N_COL)
    left_sets = left.reshape(left.shape[0], N_REP, N_COL, piece)
    right_sets = right.reshape(N_REP, N_COL, piece, right.shape[1])
    total = jnp.zeros((left.shape[0], right.shape[1]), jnp.float32)
    for group in range(N_COL):
        left_part = left_sets[:, :, group, :].reshape(left.shape[0], N_REP * piece)
        right_part = right_sets[:, group, :, :].reshape(N_REP * piece, right.shape[1])
        total = total + rounded_term(left_part, right_part)
    return total


def reference(inputs, w_in, w_out, cotangent, counts):
    token_total = (MBT * jnp.sum(counts)).astype(jnp.float32)
    positions = jnp.arange(MB * MBT, dtype=jnp.int32)
    outputs = []
    grads = []
    w_in_grad = jnp.zeros((D, FF), jnp.float32)
    w_out_grad = jnp.zeros((FF, D), jnp.float32)
    w_out_t = w_out.T
    w_in_t = w_in.T
    for replica in range(N_REP):
        tokens = inputs[replica]
        kept_mask = (positions // MBT < counts[replica]).astype(jnp.float32)
        hidden = block_sum(tokens, w_in)
        activated = gelu_tanh(hidden).astype(jnp.bfloat16)
        mixed = set_sum(activated, w_out)
        outputs.append((tokens.astype(jnp.float32) + mixed).astype(jnp.bfloat16))
        scaled = (cotangent[replica].astype(jnp.float32) * kept_mask[:, None] / token_total).astype(jnp.bfloat16)
        slope_sum = block_sum(scaled, w_out_t)
        hidden_grad = (slope_sum * gelu_slope(hidden)).astype(jnp.bfloat16)
        back = set_sum(hidden_grad, w_in_t)
        grads.append((scaled.astype(jnp.float32) + back).astype(jnp.bfloat16))
        w_in_grad = w_in_grad + jnp.dot(tokens.T, hidden_grad, preferred_element_type=jnp.float32)
        w_out_grad = w_out_grad + jnp.dot(activated.T, scaled, preferred_element_type=jnp.float32)
    return (jnp.stack(outputs), jnp.stack(grads), w_in_grad, w_out_grad)
```

```python
import jax
import jax.numpy as jnp
from jax import lax
from jax.sharding import PartitionSpec as P

MBT = 32


root_coef = 0.7978845608028654
cubic_coef = 0.044715


def gelu_tanh(values):
    inner = root_coef * (values + cubic_coef * values * values * values)
    return 0.5 * values * (1.0 + jnp.tanh(inner))


def gelu_slope(values):
    inner = root_coef * (values + cubic_coef * values * values * values)
    tangent = jnp.tanh(inner)
    return 0.5 * (1.0 + tangent) + 0.5 * values * (1.0 - tangent * tangent) * root_coef * (
        1.0 + 3.0 * cubic_coef * values * values
    )


def right_product(left, right):
    return lax.dot_general(
        left, right, (((1,), (1,)), ((), ())), preferred_element_type=jnp.float32
    )


def first_product(left, right):
    return lax.dot_general(
        left, right, (((0,), (0,)), ((), ())), preferred_element_type=jnp.float32
    )


def body(inputs, w_in, w_out, cotangent, counts):
    rows_local = inputs.shape[1]
    width_local = inputs.shape[2]
    tokens_local = inputs.reshape(rows_local, width_local)
    replicas = lax.axis_size("rep")
    replica_index = lax.axis_index("rep")
    column_index = lax.axis_index("col")
    own_count = jnp.sum(jnp.where(jnp.arange(replicas) == replica_index, counts, 0))
    token_total = (MBT * jnp.sum(counts)).astype(jnp.float32)
    positions = column_index * rows_local + jnp.arange(rows_local, dtype=jnp.int32)
    kept_mask = (positions // MBT < own_count).astype(jnp.float32)
    scaled = (
        cotangent.reshape(rows_local, width_local).astype(jnp.float32)
        * kept_mask[:, None]
        / token_total
    ).astype(jnp.bfloat16)
    tokens_all = lax.all_gather(tokens_local, ("rep", "col"), axis=0, tiled=True)
    scaled_all = lax.all_gather(scaled, ("rep", "col"), axis=0, tiled=True)
    partial_hidden = jnp.dot(tokens_all, w_in, preferred_element_type=jnp.float32)
    hidden = lax.psum_scatter(
        partial_hidden.astype(jnp.bfloat16), "row", scatter_dimension=0, tiled=True
    ).astype(jnp.float32)
    slope_terms = right_product(scaled_all, w_out)
    slope_sum = lax.psum_scatter(
        slope_terms.astype(jnp.bfloat16), "row", scatter_dimension=0, tiled=True
    ).astype(jnp.float32)
    active_share = gelu_tanh(hidden).astype(jnp.bfloat16)
    activated = lax.all_gather(active_share, "row", axis=0, tiled=True)
    grad_share = (slope_sum * gelu_slope(hidden)).astype(jnp.bfloat16)
    hidden_grad = lax.all_gather(grad_share, "row", axis=0, tiled=True)
    output_terms = jnp.dot(activated, w_out, preferred_element_type=jnp.float32)
    output_local = lax.psum_scatter(
        output_terms.astype(jnp.bfloat16), ("rep", "col"), scatter_dimension=0, tiled=True
    ).astype(jnp.float32)
    block_output = (tokens_local.astype(jnp.float32) + output_local).astype(jnp.bfloat16)
    w_out_grad = first_product(activated, scaled_all)
    back_terms = right_product(hidden_grad, w_in)
    back_local = lax.psum_scatter(
        back_terms.astype(jnp.bfloat16), ("rep", "col"), scatter_dimension=0, tiled=True
    ).astype(jnp.float32)
    input_grad = (scaled.astype(jnp.float32) + back_local).astype(jnp.bfloat16)
    w_in_grad = first_product(tokens_all, hidden_grad)
    return (
        block_output.reshape(1, rows_local, width_local),
        input_grad.reshape(1, rows_local, width_local),
        w_in_grad,
        w_out_grad,
    )


def solution(mesh):
    placed = (
        P("rep", "col", "row"),
        P("row", ("rep", "col")),
        P(("rep", "col"), "row"),
        P("rep", "col", "row"),
        P(),
    )
    return jax.shard_map(
        body,
        mesh=mesh,
        in_specs=placed,
        out_specs=(
            P("rep", "col", "row"),
            P("rep", "col", "row"),
            P("row", ("rep", "col")),
            P(("rep", "col"), "row"),
        ),
        check_vma=False,
    )
```
